256 devices in a mesh: dp: 16 (over x, z_lo, core), expert: 16 (over z_hi, y).
Axes of the slice: x: 4, y: 4, z: 8 (z_hi: 4, z_lo: 2; z = z_hi * 2 + z_lo), core: 2. Of those that a mesh axis runs over, the one named last changes fastest.
Arguments:
- tokens: bfloat16 [16, 2048, 7168], P('dp', 'expert'), may hold values from -6 to 6
- expert_ids: int32 [16, 2048, 8], P('dp', 'expert'), may hold values from 0 to 255, as said below
- slots: int32 [16, 2048, 8], P('dp', 'expert'), may hold values from 0 to 4, as said below
- route_weights: float32 [16, 2048, 8], P('dp', 'expert'), may hold values from 0.1 to 1
- w_gate: bfloat16 [16, 7168, 2048], P('expert', None, 'dp'), may hold values from -0.0625 to 0.0625
- w_up: bfloat16 [16, 7168, 2048], P('expert', None, 'dp'), may hold values from -0.0625 to 0.0625
- w_down: bfloat16 [16, 2048, 7168], P('expert', 'dp'), may hold values from -0.125 to 0.125
- readout: bfloat16 [7168], replicated, may hold values from -0.0625 to 0.0625
- ref_scores: float32 [16], replicated, may hold values from -16 to 16
- partner: int32 [16], replicated, may hold values from 0 to 15, as said below
- prompt_len: int32 [16], replicated, may hold values from 512 to 1536, as said below
Outputs:
- token_grads: bfloat16 [16, 2048, 7168], P('dp', 'expert')
- gate_grads: bfloat16 [16, 7168, 2048], P('expert', None, 'dp')
- up_grads: bfloat16 [16, 7168, 2048], P('expert', None, 'dp')
- pair_loss: float32 [16], replicated
The draws below stay inside these ranges and needn't reach their ends.
Inputs may be any that keep to these rules, and one draw needn't show every extreme that they name: `expert_ids`: each token names 8 different experts; on every row of devices along expert, one expert whose id is a multiple of 16 is chosen by every token of that row. A route gets a slot below 4 only if its expert id is a multiple of 16; within the 128 tokens of one device the routes to one such expert take slots 0, 1, 2 and so on in token order until 4 are taken, and all later routes to it get 4; every other route gets 4. partner[partner[s]] = s and partner[s] != s. `prompt_len`: the two sequences of a pair share their prompt length; some pair has 512 and some pair 3 * 512.
All inputs are finite; a program needn't handle non-finite values.
Results may differ from the reference program's by a relative error of at most 0.023.
Values may be sent and summed in bfloat16 or wider, within the bound.
No kernel may reach another device: no remote copies, remote signals or barrier semaphores. Data moves between devices by JAX's collectives and lax.ppermute only.
A program may use at most 128 MiB of HBM per device.

```python
import math
import jax
import jax.numpy as jnp
from jax import lax

D = 7168
HIDDEN_SIZE = 2048
TOPK = 8
EXP_DEV = 16
TOK_DEV = 128
DIRECTED_MODULES = 256
WIN = 16
CAP = 4
SEQ = 2048
NSEQ = 16
N_DP = 16
N_EXPERT = 16


def routing_draw(key):
    base = jax.random.fold_in(key, 11)
    key_pop, key_noise, key_hot = jax.random.split(base, 3)
    favoured_specialists = jax.random.randint(key_pop, (DIRECTED_MODULES,), 0, 2 ** 15)
    random_perturbation = jax.random.randint(key_noise, (NSEQ, SEQ, DIRECTED_MODULES), 0, 2 ** 16)
    busiest_specialist = jax.random.randint(key_hot, (NSEQ,), 0, WIN) * EXP_DEV
    complete_specialist_list = jnp.arange(DIRECTED_MODULES, dtype=jnp.int32)
    additional_increment = jnp.where(complete_specialist_list[None, :] == busiest_specialist[:, None], 2 ** 18, 0)
    rating_quantity = (random_perturbation + favoured_specialists[None, None, :] + additional_increment[:, None, :]) * DIRECTED_MODULES + complete_specialist_list[None, None, :]
    picked = lax.top_k(rating_quantity, TOPK)[1].astype(jnp.int32)
    grouped = picked.reshape(NSEQ, WIN, TOK_DEV * TOPK)
    inside = grouped % EXP_DEV == 0
    owner = grouped // EXP_DEV
    onehot = ((owner[..., None] == jnp.arange(WIN, dtype=jnp.int32)) & inside[..., None]).astype(jnp.int32)
    before = jnp.cumsum(onehot, axis=2) - onehot
    ranked = jnp.sum(before * onehot, axis=3)
    chosen = jnp.where(inside & (ranked < CAP), ranked, CAP).astype(jnp.int32)
    return (picked, chosen.reshape(NSEQ, SEQ, TOPK))


def draw_expert_ids(key, part):
    return routing_draw(key)[0]


def draw_slots(key, part):
    return routing_draw(key)[1]


def pairing_draw(key):
    base = jax.random.fold_in(key, 23)
    key_order, key_len = jax.random.split(base, 2)
    order = jax.random.permutation(key_order, NSEQ).astype(jnp.int32)
    first = order[0::2]
    second = order[1::2]
    partner = jnp.zeros((NSEQ,), jnp.int32).at[first].set(second).at[second].set(first)
    pairs = NSEQ // 2
    lens = jax.random.randint(key_len, (pairs,), SEQ // 4, 3 * SEQ // 4 + 1).astype(jnp.int32)
    lens = lens.at[0].set(SEQ // 4).at[pairs - 1].set(3 * SEQ // 4)
    length = jnp.zeros((NSEQ,), jnp.int32).at[first].set(lens).at[second].set(lens)
    return (partner, length)


def draw_partner(key, part):
    return pairing_draw(key)[0]


def draw_prompt_len(key, part):
    return pairing_draw(key)[1]


def block_scale(stream_key, dims, pieces, least, top_value):
    def one(dim, parts):
        heights = jax.random.uniform(jax.random.fold_in(jax.random.fold_in(stream_key, 6), dim), (parts,), jnp.float32, least / len(pieces), top_value / len(pieces))
        return jnp.repeat(jnp.exp(heights), dims[dim] // parts).reshape((-1,) + (1,) * (len(dims) - dim - 1))

    level = one(*pieces[0])
    for cut in pieces[1:]:
        level = level * one(*cut)
    return level


def normal_values(rng, shape, scale, limit, cuts=(), kind=jnp.bfloat16):
    drawn = jax.random.normal(rng, shape, jnp.float32) * scale
    if len(cuts) > 0:
        drawn = block_scale(rng, shape, cuts, -0.22, 0.18) * drawn
    return jnp.clip(drawn, min=-limit, max=limit).astype(kind)


def setup_inputs(seed: int = 0) -> dict:
    seeds = jax.random.split(jax.random.key(seed), 12)
    return {
        "tokens": normal_values(seeds[0], (NSEQ, SEQ, D), 1.0, 6.0, ((0, 16), (1, 16))),
        "expert_ids": draw_expert_ids(jax.random.fold_in(seeds[11], 71), 0),
        "slots": draw_slots(jax.random.fold_in(seeds[11], 71), 0),
        "route_weights": jnp.clip(jnp.exp(math.log(1.0) - 2.3025851 * jax.random.uniform(seeds[3], (NSEQ, SEQ, TOPK), jnp.float32) ** block_scale(seeds[3], (NSEQ, SEQ, TOPK), ((0, 16), (1, 16)), -0.2, 0.2)), 0.1, 1.0),
        "w_gate": normal_values(seeds[4], (WIN, D, HIDDEN_SIZE), D ** -0.5, 0.0625, ((0, 16), (2, 16))),
        "w_up": normal_values(seeds[5], (WIN, D, HIDDEN_SIZE), D ** -0.5, 0.0625, ((0, 16), (2, 16))),
        "w_down": normal_values(seeds[6], (WIN, HIDDEN_SIZE, D), HIDDEN_SIZE ** -0.5, 0.125, ((0, 16), (1, 16))),
        "readout": normal_values(seeds[7], (D,), D ** -0.5, 0.0625),
        "ref_scores": normal_values(seeds[8], (NSEQ,), 4.0, 16.0, (), jnp.float32),
        "partner": draw_partner(jax.random.fold_in(seeds[11], 71), 0),
        "prompt_len": draw_prompt_len(jax.random.fold_in(seeds[11], 71), 0),
    }


BETA = 0.1


def preference(scores, ref_scores, partner):
    count = scores.shape[0]
    order = jnp.arange(count, dtype=jnp.int32)
    diff = scores - ref_scores
    pick = (partner[:, None] == order[None, :]).astype(jnp.float32)
    other = jnp.sum(pick * diff[None, :], axis=1)
    sign = jnp.where(order < partner, 1.0, -1.0).astype(jnp.float32)
    margin = BETA * sign * (diff - other)
    return jax.nn.softplus(-margin), -BETA * sign * jax.nn.sigmoid(-margin)


def reference(tokens, expert_ids, slots, route_weights, w_gate, w_up, w_down, readout, ref_scores, partner, prompt_len):
    blocks = NSEQ * N_EXPERT
    rows = blocks * CAP
    total = WIN * rows
    ids = expert_ids.reshape(blocks, TOK_DEV * TOPK)
    chosen = slots.reshape(blocks, TOK_DEV * TOPK)
    kept = chosen < CAP
    block = jnp.arange(blocks, dtype=jnp.int32)[:, None]
    where_to = jnp.where(kept, ((ids // EXP_DEV) * blocks + block) * CAP + chosen, total).astype(jnp.int32).reshape(-1)
    source = (block * TOK_DEV + jnp.arange(TOK_DEV * TOPK, dtype=jnp.int32)[None, :] // TOPK).astype(jnp.int32).reshape(-1)
    places = jnp.arange(SEQ, dtype=jnp.int32)[None, :]
    answer = (places >= prompt_len[:, None]).astype(jnp.float32)
    scaled = (route_weights * answer[:, :, None]).reshape(-1)
    slot_source = jnp.full((total,), NSEQ * SEQ, jnp.int32).at[where_to].set(source, mode="drop")
    slot_gain = jnp.zeros((total,), jnp.float32).at[where_to].set(scaled, mode="drop")
    padded = jnp.concatenate([tokens.reshape(NSEQ * SEQ, D), jnp.zeros((1, D), jnp.bfloat16)], axis=0)
    buffer = padded[slot_source].reshape(WIN, rows, D)

    def forward(item):
        rows_w, gate_w, up_w, down_w = item
        gate = jnp.dot(rows_w, gate_w, preferred_element_type=jnp.float32)
        upper = jnp.dot(rows_w, up_w, preferred_element_type=jnp.float32)
        lever = jnp.dot(down_w, readout, preferred_element_type=jnp.float32)
        active = gate * jax.nn.sigmoid(gate)
        term = jnp.sum(active * upper * lever[None, :], axis=1)
        return gate, upper, lever, term

    gate, upper, lever, term = lax.map(forward, (buffer, w_gate, w_up, w_down))
    gains = slot_gain.reshape(WIN, NSEQ, N_EXPERT * CAP)
    scores = jnp.sum(gains * term.reshape(WIN, NSEQ, N_EXPERT * CAP), axis=(0, 2))
    losses, grads = preference(scores, ref_scores, partner)
    row_grad = (gains * grads[None, :, None]).reshape(WIN, rows)
    slice_width = HIDDEN_SIZE // N_DP

    def backward(item):
        rows_w, gate_wt, up_wt, gate_v, upper_v, lever_v, grad_v = item
        sig = jax.nn.sigmoid(gate_v)
        active = gate_v * sig
        spread = grad_v[:, None] * lever_v[None, :]
        d_gate = (spread * upper_v * sig * (1.0 + gate_v * (1.0 - sig))).astype(jnp.bfloat16)
        d_up = (spread * active).astype(jnp.bfloat16)
        grad_gate = jnp.dot(rows_w.T, d_gate, preferred_element_type=jnp.float32).astype(jnp.bfloat16)
        grad_up = jnp.dot(rows_w.T, d_up, preferred_element_type=jnp.float32).astype(jnp.bfloat16)

        def add_slice(index, acc):
            start = (index * slice_width).astype(jnp.int32)
            part = jnp.dot(lax.dynamic_slice_in_dim(d_gate, start, slice_width, 1),
                           lax.dynamic_slice_in_dim(gate_wt, start, slice_width, 1).T,
                           preferred_element_type=jnp.float32)
            part = part + jnp.dot(lax.dynamic_slice_in_dim(d_up, start, slice_width, 1),
                                  lax.dynamic_slice_in_dim(up_wt, start, slice_width, 1).T,
                                  preferred_element_type=jnp.float32)
            rounded = lax.optimization_barrier(part.astype(jnp.bfloat16))
            return acc + rounded.astype(jnp.float32)

        row_dx = lax.fori_loop(0, N_DP, add_slice, jnp.zeros((rows, D), jnp.float32)).astype(jnp.bfloat16)
        return row_dx, grad_gate, grad_up

    row_dx, gate_grads, up_grads = lax.map(backward, (buffer, w_gate, w_up, gate, upper, lever, row_grad))
    summed = jnp.zeros((NSEQ * SEQ + 1, D), jnp.float32).at[slot_source].add(row_dx.reshape(total, D).astype(jnp.float32))
    token_grads = summed[:NSEQ * SEQ].reshape(NSEQ, SEQ, D).astype(jnp.bfloat16)
    return token_grads, gate_grads, up_grads, losses
```

```python
import jax
import jax.numpy as jnp
from jax import lax
from jax.sharding import PartitionSpec as P

EXP_DEV = 16
CAP = 4
HALF = CAP // 2
PROMPT_MIN = 512
PAD = 128
BETA = 0.1


def preference(scores, ref_scores, partner):
    count = scores.shape[0]
    order = jnp.arange(count, dtype=jnp.int32)
    diff = scores - ref_scores
    pick = (partner[:, None] == order[None, :]).astype(jnp.float32)
    other = jnp.sum(pick * diff[None, :], axis=1)
    sign = jnp.where(order < partner, 1.0, -1.0).astype(jnp.float32)
    margin = BETA * sign * (diff - other)
    return (jax.nn.softplus(-margin), -BETA * sign * jax.nn.sigmoid(-margin))


def shift_x(v, step):
    return lax.ppermute(v, "dp", [(s, ((s // 4 + step) % 4) * 4 + s % 4) for s in range(16)])


def swap(v, axis, mask):
    return lax.ppermute(v, axis, [(s, s ^ mask) for s in range(16)])


def swap_z(v):
    return swap(v, "dp", 2)


def swap_core(v):
    return swap(v, "dp", 1)


def add(*parts):
    total = parts[0].astype(jnp.float32)
    for part in parts[1:]:
        total = total + part.astype(jnp.float32)
    return total.astype(jnp.bfloat16)


def gather_rows(a, b):
    za = swap_z(a)
    a_left, a_right = shift_x(a, 1), shift_x(a, -1)
    zb = swap_z(b)
    b_left, b_right = shift_x(b, 1), shift_x(b, -1)
    a_top, a_bot = shift_x(a_left[:16], 1), shift_x(a_right[16:], -1)
    za_left, za_right = swap_z(a_left), swap_z(a_right)
    zb_left, zb_right = shift_x(zb, 1), shift_x(zb, -1)
    za_top, za_bot = swap_z(a_top), swap_z(a_bot)
    b_top, b_bot = shift_x(b_left[:16], 1), shift_x(b_right[16:], -1)
    zb_top, zb_bot = shift_x(zb_left[:8], 1), shift_x(zb_right[8:], -1)
    return (
        [a, a_left, a_right, a_top, a_bot, za, za_left, za_right, za_top, za_bot],
        [b, b_left, b_right, b_top, b_bot, zb, zb_left, zb_right, zb_top, zb_bot],
    )


def ring_sum(own, left, right, far, cut):
    got_top = shift_x(far[:cut], 1)
    got_bot = shift_x(far[cut:], -1)
    to_right = jnp.concatenate([add(right[:cut], got_top), right[cut:]], axis=0)
    to_left = jnp.concatenate([left[:cut], add(left[cut:], got_bot)], axis=0)
    return own, shift_x(to_right, 1), shift_x(to_left, -1)


def reduce_rows(ya, yb):
    n = ya.shape[0] // 8
    a = [ya[i * n : (i + 1) * n] for i in range(8)]
    b = [yb[i * n : (i + 1) * n] for i in range(8)]
    far = add(a[3], swap_z(a[7]))
    left = add(a[1], swap_z(a[5]))
    right = add(a[2], swap_z(a[6]))
    other_own = swap_z(a[4])
    zown = add(*ring_sum(b[4], b[5], b[6], b[7], 8))
    bo, bl, br = ring_sum(b[0], b[1], b[2], b[3], 16)
    bz = swap_z(zown)
    ao, al, ar = ring_sum(a[0], left, right, far, 16)
    return add(ao, other_own, al, ar), add(bo, bl, br, bz)


def sum_all(v):
    for axis in ("dp", "expert"):
        for unit in (1, 4):
            one, two, three = (swap(v, axis, unit * k) for k in (1, 2, 3))
            v = (v + one) + (two + three)
    return v


def per_device(
    tokens,
    expert_ids,
    slots,
    route_weights,
    w_gate,
    w_up,
    w_down,
    readout,
    ref_scores,
    partner,
    prompt_len,
):
    n_exp = lax.axis_size("expert")
    row_index = lax.axis_index("dp")
    col_index = lax.axis_index("expert")
    acts = tokens[0]
    tok_rows, width = acts.shape
    topk = expert_ids.shape[2]
    skip = PROMPT_MIN // tok_rows * HALF
    picked = expert_ids[0].reshape(-1)
    chosen = slots[0].reshape(-1)
    route_gain = route_weights[0].reshape(-1)
    kept = chosen < CAP
    per_half = n_exp * HALF
    bucket = n_exp * CAP
    target = chosen // HALF * per_half + picked // EXP_DEV * HALF + chosen % HALF
    select = (target[None, :] == jnp.arange(bucket, dtype=jnp.int32)[:, None]) & kept[None, :]
    places = col_index * tok_rows + jnp.arange(tok_rows, dtype=jnp.int32)
    answer = (places >= prompt_len[row_index]).astype(jnp.float32)
    scaled = route_gain * jnp.repeat(answer, topk)
    slot_gain = jnp.sum(jnp.where(select, scaled[None, :], 0.0), axis=1)
    token_pick = jnp.any(select.reshape(bucket, tok_rows, topk), axis=2).astype(jnp.bfloat16)
    rows = jnp.dot(token_pick, acts, preferred_element_type=jnp.float32).astype(jnp.bfloat16)
    high = lax.reduce_precision(slot_gain, 8, 7)
    mid = lax.reduce_precision(slot_gain - high, 8, 7)
    low = slot_gain - high - mid
    lane = jnp.arange(PAD, dtype=jnp.int32)[None, :]
    parts = jnp.where(
        lane == 0, high[:, None], jnp.where(lane == 1, mid[:, None], jnp.where(lane == 2, low[:, None], 0.0))
    ).astype(jnp.bfloat16)
    outgoing = jnp.concatenate([rows, parts], axis=1)

    def to_experts(v):
        return lax.all_to_all(v, "expert", split_axis=0, concat_axis=0, tiled=True)

    block_a = to_experts(outgoing[:per_half])[skip:]
    block_b = to_experts(outgoing[per_half:])[skip:]

    half = w_gate.shape[2]
    gate_other, up_other = swap_core(w_gate[0]), swap_core(w_up[0])
    lever_own = jnp.dot(w_down[0], readout, preferred_element_type=jnp.float32)
    lever_other = swap_core(lever_own)
    w_all = jnp.concatenate([w_gate[0], w_up[0], gate_other, up_other], axis=1)

    pieces_a, pieces_b = gather_rows(block_a, block_b)
    flat = jnp.concatenate(pieces_a + pieces_b, axis=0)
    data = flat[:, :width]
    gain = jnp.sum(flat[:, width:].astype(jnp.float32), axis=1)
    projected = jnp.dot(data, w_all, preferred_element_type=jnp.float32)
    term = 0.0
    slopes = []
    for k, lever in ((0, lever_own), (1, lever_other)):
        gate = projected[:, 2 * k * half : (2 * k + 1) * half]
        upper = projected[:, (2 * k + 1) * half : (2 * k + 2) * half]
        sig = jax.nn.sigmoid(gate)
        active = gate * sig
        term = term + jnp.sum(active * upper * lever[None, :], axis=1)
        slopes.append(lever[None, :] * upper * sig * (1.0 + gate * (1.0 - sig)))
        slopes.append(lever[None, :] * active)
    slope = jnp.concatenate(slopes, axis=1)
    back = jnp.dot(slope.astype(jnp.bfloat16), w_all.T, preferred_element_type=jnp.float32).astype(jnp.bfloat16)

    steps = jnp.array([0, -1, 1, 2] * 2, dtype=jnp.int32)
    other_z = jnp.array([0] * 4 + [2] * 4, dtype=jnp.int32)
    seqs = ((row_index // 4 + steps) % 4) * 4 + ((row_index % 4) ^ other_z)
    block = block_a.shape[0]
    sums = jnp.sum((gain * term).reshape(2, 8, block), axis=(0, 2))
    order = jnp.arange(16, dtype=jnp.int32)
    onehot = (seqs[:, None] == order[None, :]).astype(jnp.float32)
    scores = sum_all(jnp.sum(onehot * sums[:, None], axis=0))
    losses, grads = preference(scores, ref_scores, partner)

    cut = 8 * block
    done_a, done_b = reduce_rows(back[:cut], back[cut:])

    block_grad = jnp.sum(onehot * grads[None, :], axis=1)
    row_grad = (gain.reshape(2, 8, block) * block_grad[None, :, None]).reshape(-1)
    d_all = (slope * row_grad[:, None]).astype(jnp.bfloat16)
    w_other = jnp.einsum("rd,rh->dh", data, d_all[:, 2 * half :], preferred_element_type=jnp.float32)
    got = swap_core(w_other.astype(jnp.bfloat16)).astype(jnp.float32)
    w_own = jnp.einsum("rd,rh->dh", data, d_all[:, : 2 * half], preferred_element_type=jnp.float32)
    total = (w_own + got).astype(jnp.bfloat16)

    empty = jnp.zeros((skip, width), jnp.bfloat16)
    home = jnp.concatenate(
        [to_experts(jnp.concatenate([empty, v], axis=0)) for v in (done_a, done_b)], axis=0
    )
    own_grad = slot_gain * grads[row_index]
    home = (home.astype(jnp.float32) * own_grad[:, None]).astype(jnp.bfloat16)
    token_grads = jnp.einsum("st,sd->td", token_pick, home, preferred_element_type=jnp.float32)
    return (token_grads.astype(jnp.bfloat16)[None], total[:, :half][None], total[:, half:][None], losses)


def solution(mesh):
    placed = (
        P("dp", "expert", None),
        P("dp", "expert", None),
        P("dp", "expert", None),
        P("dp", "expert", None),
        P("expert", None, "dp"),
        P("expert", None, "dp"),
        P("expert", "dp", None),
        P(),
        P(),
        P(),
        P(),
    )
    return jax.shard_map(
        per_device,
        mesh=mesh,
        in_specs=placed,
        out_specs=(P("dp", "expert", None), P("expert", None, "dp"), P("expert", None, "dp"), P()),
        check_vma=False,
    )
```

```python
import functools

import jax
import jax.numpy as jnp
from jax import lax
from jax.experimental import pallas as pl
from jax.experimental.pallas import tpu as pltpu
from jax.sharding import PartitionSpec as P

EXP_DEV = 16
CAP = 4
PROMPT_MIN = 512
PAD = 128
CHUNK = 1024
BETA = 0.1


def preference(scores, ref_scores, partner):
    count = scores.shape[0]
    order = jnp.arange(count, dtype=jnp.int32)
    diff = scores - ref_scores
    pick = (partner[:, None] == order[None, :]).astype(jnp.float32)
    other = jnp.sum(pick * diff[None, :], axis=1)
    sign = jnp.where(order < partner, 1.0, -1.0).astype(jnp.float32)
    margin = BETA * sign * (diff - other)
    return (jax.nn.softplus(-margin), -BETA * sign * jax.nn.sigmoid(-margin))


VMEM = functools.partial(pl.BlockSpec, memory_space=pltpu.VMEM)
SMEM = functools.partial(pl.BlockSpec, memory_space=pltpu.SMEM)


def rows_kernel(prompt, ids, slots, weights, acts, out, pick_out, gain_out):
    topk, tok_rows = ids.shape
    bucket = out.shape[0]
    width = acts.shape[1]
    shape = (bucket, tok_rows)
    position = lax.axis_index("expert") * tok_rows + lax.broadcasted_iota(jnp.int32, (1, tok_rows), 1)
    answer = (position >= prompt[lax.axis_index("dp")]).astype(jnp.float32)
    row = lax.broadcasted_iota(jnp.int32, shape, 0)
    pick = jnp.zeros(shape, jnp.float32)
    gains = jnp.zeros(shape, jnp.float32)
    for k in range(topk):
        slot = slots[k : k + 1, :]
        target = jnp.where(slot < CAP, lax.div(ids[k : k + 1, :], EXP_DEV) * CAP + slot, -1)
        hit = row == target
        pick = jnp.where(hit, 1.0, pick)
        gains = gains + jnp.where(hit, weights[k : k + 1, :] * answer, 0.0)
    gain = jnp.sum(gains, axis=1, keepdims=True)
    pick = pick.astype(jnp.bfloat16)
    pick_out[...] = pick
    gain_out[...] = jnp.broadcast_to(gain, gain_out.shape)
    out[:, :width] = jnp.dot(pick, acts[...], preferred_element_type=jnp.float32).astype(jnp.bfloat16)
    high = gain.astype(jnp.bfloat16).astype(jnp.float32)
    mid = (gain - high).astype(jnp.bfloat16).astype(jnp.float32)
    low = gain - high - mid
    lane = lax.broadcasted_iota(jnp.int32, (bucket, PAD), 1)
    parts = jnp.where(lane == 0, high, jnp.where(lane == 1, mid, jnp.where(lane == 2, low, 0.0)))
    out[:, width:] = parts.astype(jnp.bfloat16)


def whole(shape):
    return pl.BlockSpec(shape, lambda i: (0,) * len(shape))


def make_rows(prompt, ids, slots, weights, acts, bucket):
    tok_rows, width = acts.shape
    outs = [
        jax.ShapeDtypeStruct((bucket, width + PAD), jnp.bfloat16),
        jax.ShapeDtypeStruct((bucket, tok_rows), jnp.bfloat16),
        jax.ShapeDtypeStruct((bucket, 128), jnp.float32),
    ]
    return pl.pallas_call(
        rows_kernel,
        grid=(1,),
        in_specs=[SMEM()] + [whole(v.shape) for v in (ids, slots, weights, acts)],
        out_specs=[whole(v.shape) for v in outs],
        out_shape=outs,
        compiler_params=pltpu.CompilerParams(vmem_limit_bytes=16 << 20),
    )(prompt, ids, slots, weights, acts)


def sequence(place, core):
    here = lax.axis_index("dp")
    step, mask = place
    return lax.rem(lax.div(here, 4) + step + 4, 4) * 4 + (lax.rem(here, 4) ^ (mask + core))


def forward_kernel(places, *refs):
    pieces, (w, lever_own, lever_other, before) = refs[:4], refs[4:8]
    flat, own_slope, other_slope, slope16, partial, acc = refs[8:]
    n = pieces[0].shape[0]
    width = w.shape[0]
    half = w.shape[1] // 4
    for i, piece in enumerate(pieces):
        flat[i * n : (i + 1) * n, :] = piece[...]
    for k in range(0, width, CHUNK):
        part = jnp.dot(flat[:, k : k + CHUNK], w[k : k + CHUNK, :], preferred_element_type=jnp.float32)
        acc[...] = part if k == 0 else acc[...] + part
    gain = jnp.sum(flat[:, width:].astype(jnp.float32), axis=1, keepdims=True)
    term = 0.0
    for k, lever_ref, out in ((0, lever_own, own_slope), (1, lever_other, other_slope)):
        lever = lever_ref[...]
        gate = acc[:, 2 * k * half : (2 * k + 1) * half]
        upper = acc[:, (2 * k + 1) * half : (2 * k + 2) * half]
        sig = jax.nn.sigmoid(gate)
        active = gate * sig
        term = term + jnp.sum(active * upper * lever, axis=1, keepdims=True)
        d_gate = lever * upper * sig * (1.0 + gate * (1.0 - sig))
        d_up = lever * active
        out[:, :half] = d_gate
        out[:, half:] = d_up
        slope16[:, 2 * k * half : (2 * k + 1) * half] = d_gate.astype(jnp.bfloat16)
        slope16[:, (2 * k + 1) * half : (2 * k + 2) * half] = d_up.astype(jnp.bfloat16)
    scored = gain * term
    lane = lax.broadcasted_iota(jnp.int32, (1, 128), 1)
    total = before[...]
    h = n // 2
    for i, place in enumerate(places):
        block = jnp.sum(scored[i * h : (i + 1) * h, :], axis=0, keepdims=True)
        total = total + jnp.where(lane == sequence(place, 0), block, 0.0)
    partial[...] = total


def forward(places, pieces, w, lever_own, lever_other, before):
    n, padded = pieces[0].shape
    rows, half = 4 * n, w.shape[1] // 4
    return pl.pallas_call(
        functools.partial(forward_kernel, places),
        in_specs=[VMEM() for _ in range(8)],
        out_specs=[VMEM() for _ in range(5)],
        out_shape=[
            jax.ShapeDtypeStruct((rows, padded), jnp.bfloat16),
            jax.ShapeDtypeStruct((rows, 2 * half), jnp.float32),
            jax.ShapeDtypeStruct((rows, 2 * half), jnp.float32),
            jax.ShapeDtypeStruct((rows, 4 * half), jnp.bfloat16),
            jax.ShapeDtypeStruct((1, 128), jnp.float32),
        ],
        scratch_shapes=[pltpu.VMEM((rows, 4 * half), jnp.float32)],
        compiler_params=pltpu.CompilerParams(vmem_limit_bytes=32 << 20),
    )(*pieces, w, lever_own, lever_other, before)


def back_kernel(slope, w, *outs):
    for k in range(0, w.shape[0], CHUNK):
        y = lax.dot_general(
            slope[...], w[k : k + CHUNK, :], (((1,), (1,)), ((), ())), preferred_element_type=jnp.float32
        )
        start = 0
        for out in outs:
            out[:, k : k + CHUNK] = y[start : start + out.shape[0], :].astype(jnp.bfloat16)
            start += out.shape[0]


def back(slope, w, sizes):
    return pl.pallas_call(
        back_kernel,
        in_specs=[VMEM(), VMEM()],
        out_specs=[VMEM() for _ in sizes],
        out_shape=[jax.ShapeDtypeStruct((n, w.shape[0]), jnp.bfloat16) for n in sizes],
        compiler_params=pltpu.CompilerParams(vmem_limit_bytes=32 << 20),
    )(slope, w)


def weights_kernel(sources, grads, *refs):
    count = len(sources)
    rows, gains, slopes = refs[:count], refs[count : 2 * count], refs[2 * count : 3 * count]
    gate_out, up_out, scaled = refs[3 * count :]
    half = gate_out.shape[1]

    @pl.when(pl.program_id(0) == 0)
    def _():
        for j, (places, core) in enumerate(sources):
            gain = jnp.sum(gains[j][...].astype(jnp.float32), axis=1, keepdims=True)
            h = gain.shape[0] // len(places)
            factor = jnp.concatenate(
                [gain[i * h : (i + 1) * h, :] * grads[sequence(place, core)] for i, place in enumerate(places)], axis=0
            )
            scaled[j] = (slopes[j][...] * factor).astype(jnp.bfloat16)

    total = jnp.zeros((gate_out.shape[0], 2 * half), jnp.float32)
    for j in range(count):
        total = total + lax.dot_general(
            rows[j][...], scaled[j], (((0,), (0,)), ((), ())), preferred_element_type=jnp.float32
        )
    gate_out[...] = total[:, :half].astype(jnp.bfloat16)
    up_out[...] = total[:, half:].astype(jnp.bfloat16)


def weight_grads(sources, rows, slopes, grads, width, half):
    n = rows[0].shape[0]
    last = width // PAD
    return pl.pallas_call(
        functools.partial(weights_kernel, sources),
        grid=(width // CHUNK,),
        in_specs=[SMEM()]
        + [pl.BlockSpec((n, CHUNK), lambda i: (0, i)) for _ in rows]
        + [pl.BlockSpec((n, PAD), lambda i: (0, last)) for _ in rows]
        + [pl.BlockSpec((n, 2 * half), lambda i: (0, 0)) for _ in slopes],
        out_specs=[pl.BlockSpec((CHUNK, half), lambda i: (i, 0)) for _ in range(2)],
        out_shape=[jax.ShapeDtypeStruct((width, half), jnp.bfloat16) for _ in range(2)],
        scratch_shapes=[pltpu.VMEM((len(rows), n, 2 * half), jnp.bfloat16)],
        compiler_params=pltpu.CompilerParams(vmem_limit_bytes=16 << 20),
    )(grads, *rows, *rows, *slopes)


def shift_x(v, step):
    return lax.ppermute(v, "dp", [(s, ((s // 4 + step) % 4) * 4 + s % 4) for s in range(16)])


def swap(v, axis, mask):
    return lax.ppermute(v, axis, [(s, s ^ mask) for s in range(16)])


def swap_z(v):
    return swap(v, "dp", 2)


def swap_core(v):
    return swap(v, "dp", 1)


def add(*parts):
    total = parts[0].astype(jnp.float32)
    for part in parts[1:]:
        total = total + part.astype(jnp.float32)
    return total.astype(jnp.bfloat16)


def gather_rows(own):
    h = own.shape[0] // 2
    left, right, zown = shift_x(own, 1), shift_x(own, -1), swap_z(own)
    left, right, zown = lax.optimization_barrier((left, right, zown))
    first = [own, left, right, zown]
    plus = shift_x(jnp.concatenate([left[:h], zown[h:]], axis=0), 1)
    minus = shift_x(jnp.concatenate([right[h:], zown[:h]], axis=0), -1)
    across = swap_z(jnp.concatenate([left[:h], right[h:]], axis=0))
    plus, minus, across = lax.optimization_barrier((plus, minus, across))
    zfar0 = shift_x(across[:h], 1)
    zfar1 = shift_x(across[h:], -1)
    zfar0, zfar1 = lax.optimization_barrier((zfar0, zfar1))
    return first, [plus, minus, across, jnp.concatenate([zfar0, zfar1], axis=0)]


def reduce_rows(make_first, second, later):
    plus, minus, across, zfar0, zfar1 = second
    h = zfar0.shape[0]
    got0 = shift_x(zfar0, -1)
    got1 = shift_x(zfar1, 1)
    got_plus = shift_x(plus, -1)
    got_minus = shift_x(minus, 1)
    across = add(across, jnp.concatenate([got0, got1], axis=0))
    across, later = lax.optimization_barrier((across, later))
    got_across = swap_z(across)
    own, left, right, zown = make_first(across)
    later = sum_over(later, "dp")
    got_plus, got_minus, got_across = lax.optimization_barrier((got_plus, got_minus, got_across))
    zown = jnp.concatenate([add(zown[:h], got_minus[h:]), add(zown[h:], got_plus[h:])], axis=0)
    left = jnp.concatenate([add(left[:h], got_plus[:h], got_across[:h]), left[h:]], axis=0)
    right = jnp.concatenate([right[:h], add(right[h:], got_minus[:h], got_across[h:])], axis=0)
    left, right, zown, later = lax.optimization_barrier((left, right, zown, later))
    return add(own, *lax.optimization_barrier((swap_z(zown), shift_x(left, -1), shift_x(right, 1)))), later


FIRST = ((0, 0), (0, 0), (-1, 0), (-1, 0), (1, 0), (1, 0), (0, 2), (0, 2))
SECOND = ((2, 0), (-1, 2), (2, 0), (1, 2), (-1, 2), (1, 2), (2, 2), (2, 2))


def sum_over(v, axis):
    for unit in (1, 4):
        one, two, three = (swap(v, axis, unit * k) for k in (1, 2, 3))
        v = (v + one) + (two + three)
    return v


def per_device(
    tokens,
    expert_ids,
    slots,
    route_weights,
    w_gate,
    w_up,
    w_down,
    readout,
    ref_scores,
    partner,
    prompt_len,
):
    n_exp = lax.axis_size("expert")
    row_index = lax.axis_index("dp")
    acts = tokens[0]
    tok_rows, width = acts.shape
    skip = PROMPT_MIN // tok_rows * CAP
    outgoing, token_pick, slot_gain = make_rows(
        prompt_len, expert_ids[0].T, slots[0].T, route_weights[0].T, acts, n_exp * CAP
    )

    def to_experts(v):
        return lax.all_to_all(v, "expert", split_axis=0, concat_axis=0, tiled=True)

    mine = to_experts(outgoing)[skip:]

    half = w_gate.shape[2]
    gate_other, up_other = swap_core(w_gate[0]), swap_core(w_up[0])
    lever_own = jnp.dot(w_down[0], readout, preferred_element_type=jnp.float32)
    lever_own = lever_own.reshape(1, half)
    lever_other = swap_core(lever_own)
    w_all = jnp.concatenate([w_gate[0], w_up[0], gate_other, up_other], axis=1)

    pieces = gather_rows(mine)
    unit = mine.shape[0]
    partial = jnp.zeros((1, 128), jnp.float32)
    slopes16, sources, rows, slopes = [], [], [], []
    for some, places in zip(pieces, (FIRST, SECOND)):
        flat, own_slope, other_slope, slope16, partial = forward(places, some, w_all, lever_own, lever_other, partial)
        slopes16.append(slope16)
        sources += [(places, 0), (places, 1)]
        rows += [flat, swap_core(flat)]
        slopes += [own_slope, swap_core(other_slope)]

    def make_first(after):
        slope, _ = lax.optimization_barrier((slopes16[0], after))
        return back(slope, w_all, [unit] * 4)

    done, partial = reduce_rows(make_first, back(slopes16[1], w_all, [unit] * 3 + [unit // 2] * 2), partial)
    scores = sum_over(partial, "expert")[0, : partner.shape[0]]
    losses, grads = preference(scores, ref_scores, partner)
    gate_grads, up_grads = weight_grads(sources, rows, slopes, grads, width, half)

    empty = jnp.zeros((skip, width), jnp.bfloat16)
    home = to_experts(jnp.concatenate([empty, done], axis=0))
    home, gate_grads, up_grads = lax.optimization_barrier((home, gate_grads, up_grads))
    own_grad = slot_gain[:, 0] * grads[row_index]
    home = (home.astype(jnp.float32) * own_grad[:, None]).astype(jnp.bfloat16)
    token_grads = jnp.einsum("st,sd->td", token_pick, home, preferred_element_type=jnp.float32)
    return (token_grads.astype(jnp.bfloat16)[None], gate_grads[None], up_grads[None], losses)


def solution(mesh):
    placed = (
        P("dp", "expert", None),
        P("dp", "expert", None),
        P("dp", "expert", None),
        P("dp", "expert", None),
        P("expert", None, "dp"),
        P("expert", None, "dp"),
        P("expert", "dp", None),
        P(),
        P(),
        P(),
        P(),
    )
    return jax.shard_map(
        per_device,
        mesh=mesh,
        in_specs=placed,
        out_specs=(P("dp", "expert", None), P("expert", None, "dp"), P("expert", None, "dp"), P()),
        check_vma=False,
    )
```

```python
import functools

import jax
import jax.numpy as jnp
from jax import lax
from jax.experimental import pallas as pl
from jax.experimental.pallas import tpu as pltpu
from jax.sharding import PartitionSpec as P

EXP_DEV = 16
CAP = 4
PROMPT_MIN = 512
PAD = 128
CHUNK = 1024
BETA = 0.1


def preference(scores, ref_scores, partner):
    count = scores.shape[0]
    order = jnp.arange(count, dtype=jnp.int32)
    diff = scores - ref_scores
    pick = (partner[:, None] == order[None, :]).astype(jnp.float32)
    other = jnp.sum(pick * diff[None, :], axis=1)
    sign = jnp.where(order < partner, 1.0, -1.0).astype(jnp.float32)
    margin = BETA * sign * (diff - other)
    return (jax.nn.softplus(-margin), -BETA * sign * jax.nn.sigmoid(-margin))


VMEM = functools.partial(pl.BlockSpec, memory_space=pltpu.VMEM)
SMEM = functools.partial(pl.BlockSpec, memory_space=pltpu.SMEM)


def rows_kernel(prompt, ids_in, slots_in, weights_in, acts_in, out, pick_out, gain_out, *scratch):
    ids, slots, weights, acts, total, sems = scratch
    copies = [
        pltpu.make_async_copy(source, target, sems.at[i])
        for i, (source, target) in enumerate(((ids_in, ids), (slots_in, slots), (weights_in, weights), (acts_in, acts)))
    ]
    for copy in copies:
        copy.start()
    for copy in copies[:3]:
        copy.wait()
    topk, tok_rows = ids.shape
    bucket = pick_out.shape[0]
    width = acts.shape[1]
    shape = (bucket, tok_rows)
    position = lax.axis_index("expert") * tok_rows + lax.broadcasted_iota(jnp.int32, (1, tok_rows), 1)
    answer = (position >= prompt[lax.axis_index("dp")]).astype(jnp.float32)
    row = lax.broadcasted_iota(jnp.int32, shape, 0)
    pick = jnp.zeros(shape, jnp.float32)
    gains = jnp.zeros(shape, jnp.float32)
    for k in range(topk):
        slot = slots[k : k + 1, :]
        target = jnp.where(slot < CAP, lax.div(ids[k : k + 1, :], EXP_DEV) * CAP + slot, -1)
        hit = row == target
        pick = jnp.where(hit, 1.0, pick)
        gains = gains + jnp.where(hit, weights[k : k + 1, :] * answer, 0.0)
    gain = jnp.sum(gains, axis=1, keepdims=True)
    pick = pick.astype(jnp.bfloat16)
    pick_out[...] = pick
    gain_out[...] = jnp.broadcast_to(gain, gain_out.shape)
    copies[3].wait()
    total[:, :width] = jnp.dot(pick, acts[...], preferred_element_type=jnp.float32)
    high = gain.astype(jnp.bfloat16).astype(jnp.float32)
    mid = (gain - high).astype(jnp.bfloat16).astype(jnp.float32)
    low = gain - high - mid
    lane = lax.broadcasted_iota(jnp.int32, (bucket, PAD), 1)
    parts = jnp.where(lane == 0, high, jnp.where(lane == 1, mid, jnp.where(lane == 2, low, 0.0)))
    total[:, width:] = parts
    for i in range(out.shape[0]):
        out[i] = total[i * CAP : (i + 1) * CAP, :].astype(jnp.bfloat16)


def make_rows(prompt, ids, slots, weights, acts, bucket):
    tok_rows, width = acts.shape
    outs = [
        jax.ShapeDtypeStruct((bucket // CAP, CAP, width + PAD), jnp.bfloat16),
        jax.ShapeDtypeStruct((bucket, tok_rows), jnp.bfloat16),
        jax.ShapeDtypeStruct((bucket, 128), jnp.float32),
    ]
    ids, slots, weights, acts = (
        pltpu.with_memory_space_constraint(v, pltpu.HBM) for v in (ids, slots, weights, acts)
    )
    return pl.pallas_call(
        rows_kernel,
        in_specs=[SMEM()] + [pl.BlockSpec(memory_space=pltpu.HBM) for _ in range(4)],
        out_specs=[VMEM() for _ in outs],
        out_shape=outs,
        scratch_shapes=[pltpu.VMEM(v.shape, v.dtype) for v in (ids, slots, weights, acts)]
        + [pltpu.VMEM((bucket, width + PAD), jnp.float32), pltpu.SemaphoreType.DMA((4,))],
        compiler_params=pltpu.CompilerParams(vmem_limit_bytes=16 << 20),
    )(prompt, ids, slots, weights, acts)


def pack_kernel(own, a, b, c, out, total):
    blocks, n, _ = out.shape
    total[...] = (
        own[...].astype(jnp.float32)
        + a[...].astype(jnp.float32)
        + b[...].astype(jnp.float32)
        + c[...].astype(jnp.float32)
    )
    skip = blocks - total.shape[0] // n
    for i in range(blocks):
        if i < skip:
            out[i] = jnp.zeros(out.shape[1:], jnp.bfloat16)
        else:
            out[i] = total[(i - skip) * n : (i - skip + 1) * n, :].astype(jnp.bfloat16)


def pack(own, *others):
    rows, width = own.shape
    blocks = lax.axis_size("expert")
    return pl.pallas_call(
        pack_kernel,
        in_specs=[VMEM() for _ in range(4)],
        out_specs=VMEM(),
        out_shape=jax.ShapeDtypeStruct((blocks, CAP, width), jnp.bfloat16),
        scratch_shapes=[pltpu.VMEM((rows, width), jnp.float32)],
        compiler_params=pltpu.CompilerParams(vmem_limit_bytes=16 << 20),
    )(own, *others)


def unpack_kernel(blocks, out, total):
    n = blocks.shape[1]
    skip = blocks.shape[0] - out.shape[0] // n
    for i in range(skip, blocks.shape[0]):
        total[(i - skip) * n : (i - skip + 1) * n, :] = blocks[i].astype(jnp.float32)
    out[...] = total[...].astype(jnp.bfloat16)


def unpack(blocks, rows):
    width = blocks.shape[2]
    return pl.pallas_call(
        unpack_kernel,
        in_specs=[VMEM()],
        out_specs=VMEM(),
        out_shape=jax.ShapeDtypeStruct((rows, width), jnp.bfloat16),
        scratch_shapes=[pltpu.VMEM((rows, width), jnp.float32)],
        compiler_params=pltpu.CompilerParams(vmem_limit_bytes=16 << 20),
    )(blocks)


def home_kernel(grads, pick, gain, blocks, out, total):
    n = blocks.shape[1]
    factor = gain[:, :1] * grads[lax.axis_index("dp")]
    for i in range(blocks.shape[0]):
        total[i * n : (i + 1) * n, :] = blocks[i].astype(jnp.float32)
    for k in range(0, out.shape[1], CHUNK):
        rows = (total[:, k : k + CHUNK] * factor).astype(jnp.bfloat16)
        grad = lax.dot_general(pick[...], rows, (((0,), (0,)), ((), ())), preferred_element_type=jnp.float32)
        out[:, k : k + CHUNK] = grad.astype(jnp.bfloat16)


def to_tokens(grads, pick, gain, blocks):
    width = blocks.shape[2]
    return pl.pallas_call(
        home_kernel,
        in_specs=[SMEM(), VMEM(), VMEM(), VMEM()],
        out_specs=VMEM(),
        out_shape=jax.ShapeDtypeStruct((pick.shape[1], width), jnp.bfloat16),
        scratch_shapes=[pltpu.VMEM((pick.shape[0], width), jnp.float32)],
        compiler_params=pltpu.CompilerParams(vmem_limit_bytes=16 << 20),
    )(grads, pick, gain, blocks)


def sequence(place, core):
    here = lax.axis_index("dp")
    step, mask = place
    return lax.rem(lax.div(here, 4) + step + 4, 4) * 4 + (lax.rem(here, 4) ^ (mask + core))


def forward_kernel(places, *refs):
    pieces, (w, lever_own, lever_other, before) = refs[:4], refs[4:8]
    flat, own_slope, other_slope, slope16, partial, acc = refs[8:]
    n = pieces[0].shape[0]
    width = w.shape[0]
    half = w.shape[1] // 4
    for i, piece in enumerate(pieces):
        flat[i * n : (i + 1) * n, :] = piece[...]
    for k in range(0, width, CHUNK):
        part = jnp.dot(flat[:, k : k + CHUNK], w[k : k + CHUNK, :], preferred_element_type=jnp.float32)
        acc[...] = part if k == 0 else acc[...] + part
    gain = jnp.sum(flat[:, width:].astype(jnp.float32), axis=1, keepdims=True)
    term = 0.0
    for k, lever_ref, out in ((0, lever_own, own_slope), (1, lever_other, other_slope)):
        lever = lever_ref[...]
        gate = acc[:, 2 * k * half : (2 * k + 1) * half]
        upper = acc[:, (2 * k + 1) * half : (2 * k + 2) * half]
        sig = jax.nn.sigmoid(gate)
        active = gate * sig
        term = term + jnp.sum(active * upper * lever, axis=1, keepdims=True)
        d_gate = lever * upper * sig * (1.0 + gate * (1.0 - sig))
        d_up = lever * active
        out[:, :half] = d_gate
        out[:, half:] = d_up
        slope16[:, 2 * k * half : (2 * k + 1) * half] = d_gate.astype(jnp.bfloat16)
        slope16[:, (2 * k + 1) * half : (2 * k + 2) * half] = d_up.astype(jnp.bfloat16)
    scored = gain * term
    lane = lax.broadcasted_iota(jnp.int32, (1, 128), 1)
    total = before[...]
    h = n // 2
    for i, place in enumerate(places):
        block = jnp.sum(scored[i * h : (i + 1) * h, :], axis=0, keepdims=True)
        total = total + jnp.where(lane == sequence(place, 0), block, 0.0)
    partial[...] = total


def forward(places, pieces, w, lever_own, lever_other, before):
    n, padded = pieces[0].shape
    rows, half = 4 * n, w.shape[1] // 4
    return pl.pallas_call(
        functools.partial(forward_kernel, places),
        in_specs=[VMEM() for _ in range(8)],
        out_specs=[VMEM() for _ in range(5)],
        out_shape=[
            jax.ShapeDtypeStruct((rows, padded), jnp.bfloat16),
            jax.ShapeDtypeStruct((rows, 2 * half), jnp.float32),
            jax.ShapeDtypeStruct((rows, 2 * half), jnp.float32),
            jax.ShapeDtypeStruct((rows, 4 * half), jnp.bfloat16),
            jax.ShapeDtypeStruct((1, 128), jnp.float32),
        ],
        scratch_shapes=[pltpu.VMEM((rows, 4 * half), jnp.float32)],
        compiler_params=pltpu.CompilerParams(vmem_limit_bytes=32 << 20),
    )(*pieces, w, lever_own, lever_other, before)


def back_kernel(slope, w, *outs):
    for k in range(0, w.shape[0], CHUNK):
        y = lax.dot_general(
            slope[...], w[k : k + CHUNK, :], (((1,), (1,)), ((), ())), preferred_element_type=jnp.float32
        )
        start = 0
        for out in outs:
            out[:, k : k + CHUNK] = y[start : start + out.shape[0], :].astype(jnp.bfloat16)
            start += out.shape[0]


def back(slope, w, sizes):
    return pl.pallas_call(
        back_kernel,
        in_specs=[VMEM(), VMEM()],
        out_specs=[VMEM() for _ in sizes],
        out_shape=[jax.ShapeDtypeStruct((n, w.shape[0]), jnp.bfloat16) for n in sizes],
        compiler_params=pltpu.CompilerParams(vmem_limit_bytes=32 << 20),
    )(slope, w)


def weights_kernel(sources, grads, *refs):
    count = len(sources)
    rows, gains, slopes = refs[:count], refs[count : 2 * count], refs[2 * count : 3 * count]
    gate_out, up_out, scaled = refs[3 * count :]
    half = gate_out.shape[1]

    @pl.when(pl.program_id(0) == 0)
    def _():
        for j, (places, core) in enumerate(sources):
            gain = jnp.sum(gains[j][...].astype(jnp.float32), axis=1, keepdims=True)
            h = gain.shape[0] // len(places)
            factor = jnp.concatenate(
                [gain[i * h : (i + 1) * h, :] * grads[sequence(place, core)] for i, place in enumerate(places)], axis=0
            )
            scaled[j] = (slopes[j][...] * factor).astype(jnp.bfloat16)

    total = jnp.zeros((gate_out.shape[0], 2 * half), jnp.float32)
    for j in range(count):
        total = total + lax.dot_general(
            rows[j][...], scaled[j], (((0,), (0,)), ((), ())), preferred_element_type=jnp.float32
        )
    gate_out[...] = total[:, :half].astype(jnp.bfloat16)
    up_out[...] = total[:, half:].astype(jnp.bfloat16)


def weight_grads(sources, rows, slopes, grads, width, half):
    n = rows[0].shape[0]
    last = width // PAD
    return pl.pallas_call(
        functools.partial(weights_kernel, sources),
        grid=(width // CHUNK,),
        in_specs=[SMEM()]
        + [pl.BlockSpec((n, CHUNK), lambda i: (0, i)) for _ in rows]
        + [pl.BlockSpec((n, PAD), lambda i: (0, last)) for _ in rows]
        + [pl.BlockSpec((n, 2 * half), lambda i: (0, 0)) for _ in slopes],
        out_specs=[pl.BlockSpec((CHUNK, half), lambda i: (i, 0)) for _ in range(2)],
        out_shape=[jax.ShapeDtypeStruct((width, half), jnp.bfloat16) for _ in range(2)],
        scratch_shapes=[pltpu.VMEM((len(rows), n, 2 * half), jnp.bfloat16)],
        compiler_params=pltpu.CompilerParams(vmem_limit_bytes=16 << 20),
    )(grads, *rows, *rows, *slopes)


def shift_x(v, step):
    return lax.ppermute(v, "dp", [(s, ((s // 4 + step) % 4) * 4 + s % 4) for s in range(16)])


def swap(v, axis, mask):
    return lax.ppermute(v, axis, [(s, s ^ mask) for s in range(16)])


def swap_z(v):
    return swap(v, "dp", 2)


def swap_core(v):
    return swap(v, "dp", 1)


def add(*parts):
    total = parts[0].astype(jnp.float32)
    for part in parts[1:]:
        total = total + part.astype(jnp.float32)
    return total.astype(jnp.bfloat16)


def sum_step(v, axis, unit):
    one, two, three = (swap(v, axis, unit * k) for k in (1, 2, 3))
    return (v + one) + (two + three)


def gather_rows(own):
    h = own.shape[0] // 2
    left, right, zown = shift_x(own, 1), shift_x(own, -1), swap_z(own)
    left, right, zown = lax.optimization_barrier((left, right, zown))
    first = [own, left, right, zown]
    plus = shift_x(jnp.concatenate([left[:h], zown[h:]], axis=0), 1)
    minus = shift_x(jnp.concatenate([right[h:], zown[:h]], axis=0), -1)
    across = swap_z(jnp.concatenate([left[:h], right[h:]], axis=0))
    plus, minus, across = lax.optimization_barrier((plus, minus, across))
    zfar0 = shift_x(across[:h], 1)
    zfar1 = shift_x(across[h:], -1)
    zfar0, zfar1 = lax.optimization_barrier((zfar0, zfar1))
    return first, [plus, minus, across, jnp.concatenate([zfar0, zfar1], axis=0)]


def reduce_rows(make_first, second, later):
    plus, minus, across, zfar0, zfar1 = second
    h = zfar0.shape[0]
    zfar0, zfar1, later = lax.optimization_barrier((zfar0, zfar1, later))
    got0 = shift_x(zfar0, -1)
    got1 = shift_x(zfar1, 1)
    got_plus = shift_x(plus, -1)
    got_minus = shift_x(minus, 1)
    later = sum_step(later, "dp", 1)
    got0, got1, later = lax.optimization_barrier((got0, got1, later))
    across = add(across, jnp.concatenate([got0, got1], axis=0))
    across, later = lax.optimization_barrier((across, later))
    later = sum_step(later, "expert", 1)
    got_across = swap_z(across)
    own, left, right, zown = make_first(across)
    got_plus, got_minus, got_across = lax.optimization_barrier((got_plus, got_minus, got_across))
    zown = jnp.concatenate([add(zown[:h], got_minus[h:]), add(zown[h:], got_plus[h:])], axis=0)
    left = jnp.concatenate([add(left[:h], got_plus[:h], got_across[:h]), left[h:]], axis=0)
    right = jnp.concatenate([right[:h], add(right[h:], got_minus[:h], got_across[h:])], axis=0)
    left, right, zown, later = lax.optimization_barrier((left, right, zown, later))
    later = sum_step(later, "expert", 4)
    sums = lax.optimization_barrier((swap_z(zown), shift_x(left, -1), shift_x(right, 1), later))
    return pack(own, *sums[:3]), sums[3]


FIRST = ((0, 0), (0, 0), (-1, 0), (-1, 0), (1, 0), (1, 0), (0, 2), (0, 2))
SECOND = ((2, 0), (-1, 2), (2, 0), (1, 2), (-1, 2), (1, 2), (2, 2), (2, 2))


def per_device(
    tokens,
    expert_ids,
    slots,
    route_weights,
    w_gate,
    w_up,
    w_down,
    readout,
    ref_scores,
    partner,
    prompt_len,
):
    n_exp = lax.axis_size("expert")
    row_index = lax.axis_index("dp")
    acts = tokens[0]
    tok_rows, width = acts.shape
    outgoing, token_pick, slot_gain = make_rows(
        prompt_len, expert_ids[0].T, slots[0].T, route_weights[0].T, acts, n_exp * CAP
    )

    def to_experts(v):
        return lax.all_to_all(v, "expert", split_axis=0, concat_axis=0, tiled=True)

    mine = unpack(to_experts(outgoing), (n_exp - PROMPT_MIN // tok_rows) * CAP)

    half = w_gate.shape[2]
    gate_other, up_other = swap_core(w_gate[0]), swap_core(w_up[0])
    lever_own = jnp.dot(w_down[0], readout, preferred_element_type=jnp.float32)
    lever_own = lever_own.reshape(1, half)
    lever_other = swap_core(lever_own)
    w_all = jnp.concatenate([w_gate[0], w_up[0], gate_other, up_other], axis=1)

    pieces = gather_rows(mine)
    unit = mine.shape[0]
    partial = jnp.zeros((1, 128), jnp.float32)
    slopes16, sources, rows, slopes = [], [], [], []
    for some, places in zip(pieces, (FIRST, SECOND)):
        flat, own_slope, other_slope, slope16, partial = forward(places, some, w_all, lever_own, lever_other, partial)
        slopes16.append(slope16)
        sources += [(places, 0), (places, 1)]
        rows += [flat, swap_core(flat)]
        slopes += [own_slope, swap_core(other_slope)]

    def make_first(after):
        slope, _ = lax.optimization_barrier((slopes16[0], after))
        return back(slope, w_all, [unit] * 4)

    packed, partial = reduce_rows(make_first, back(slopes16[1], w_all, [unit] * 3 + [unit // 2] * 2), partial)
    packed, later = lax.optimization_barrier((packed, partial))
    scores = sum_step(later, "dp", 4)[0, : partner.shape[0]]
    losses, grads = preference(scores, ref_scores, partner)
    gate_grads, up_grads = weight_grads(sources, rows, slopes, grads, width, half)
    home, gate_grads, up_grads = lax.optimization_barrier((to_experts(packed), gate_grads, up_grads))
    token_grads = to_tokens(grads, token_pick, slot_gain, home)
    return (token_grads[None], gate_grads[None], up_grads[None], losses)


def solution(mesh):
    placed = (
        P("dp", "expert", None),
        P("dp", "expert", None),
        P("dp", "expert", None),
        P("dp", "expert", None),
        P("expert", None, "dp"),
        P("expert", None, "dp"),
        P("expert", "dp", None),
        P(),
        P(),
        P(),
        P(),
    )
    return jax.shard_map(
        per_device,
        mesh=mesh,
        in_specs=placed,
        out_specs=(P("dp", "expert", None), P("expert", None, "dp"), P("expert", None, "dp"), P()),
        check_vma=False,
    )
```

```python
import functools

import jax
import jax.numpy as jnp
from jax import lax
from jax.experimental import pallas as pl
from jax.experimental.pallas import tpu as pltpu
from jax.sharding import PartitionSpec as P

EXP_DEV = 16
CAP = 4
PROMPT_MIN = 512
PAD = 128
CHUNK = 1024
BETA = 0.1


def preference(scores, ref_scores, partner):
    count = scores.shape[0]
    order = jnp.arange(count, dtype=jnp.int32)
    diff = scores - ref_scores
    pick = (partner[:, None] == order[None, :]).astype(jnp.float32)
    other = jnp.sum(pick * diff[None, :], axis=1)
    sign = jnp.where(order < partner, 1.0, -1.0).astype(jnp.float32)
    margin = BETA * sign * (diff - other)
    return (jax.nn.softplus(-margin), -BETA * sign * jax.nn.sigmoid(-margin))


VMEM = functools.partial(pl.BlockSpec, memory_space=pltpu.VMEM)
SMEM = functools.partial(pl.BlockSpec, memory_space=pltpu.SMEM)


def rows_kernel(prompt, ids_in, slots_in, weights_in, acts_in, out, pick_out, gain_out, *scratch):
    ids, slots, weights, acts, total, sems = scratch
    copies = [
        pltpu.make_async_copy(source, target, sems.at[i])
        for i, (source, target) in enumerate(((ids_in, ids), (slots_in, slots), (weights_in, weights), (acts_in, acts)))
    ]
    for copy in copies:
        copy.start()
    for copy in copies[:3]:
        copy.wait()
    topk, tok_rows = ids.shape
    bucket = pick_out.shape[0]
    width = acts.shape[1]
    shape = (bucket, tok_rows)
    position = lax.axis_index("expert") * tok_rows + lax.broadcasted_iota(jnp.int32, (1, tok_rows), 1)
    answer = (position >= prompt[lax.axis_index("dp")]).astype(jnp.float32)
    row = lax.broadcasted_iota(jnp.int32, shape, 0)
    pick = jnp.zeros(shape, jnp.float32)
    gains = jnp.zeros(shape, jnp.float32)
    for k in range(topk):
        slot = slots[k : k + 1, :]
        target = jnp.where(slot < CAP, lax.div(ids[k : k + 1, :], EXP_DEV) * CAP + slot, -1)
        hit = row == target
        pick = jnp.where(hit, 1.0, pick)
        gains = gains + jnp.where(hit, weights[k : k + 1, :] * answer, 0.0)
    gain = jnp.sum(gains, axis=1, keepdims=True)
    pick = pick.astype(jnp.bfloat16)
    pick_out[...] = pick
    gain_out[...] = jnp.broadcast_to(gain, gain_out.shape)
    copies[3].wait()
    total[:, :width] = jnp.dot(pick, acts[...], preferred_element_type=jnp.float32)
    high = gain.astype(jnp.bfloat16).astype(jnp.float32)
    mid = (gain - high).astype(jnp.bfloat16).astype(jnp.float32)
    low = gain - high - mid
    lane = lax.broadcasted_iota(jnp.int32, (bucket, PAD), 1)
    parts = jnp.where(lane == 0, high, jnp.where(lane == 1, mid, jnp.where(lane == 2, low, 0.0)))
    total[:, width:] = parts
    for i in range(out.shape[0]):
        out[i] = total[i * CAP : (i + 1) * CAP, :].astype(jnp.bfloat16)


def make_rows(prompt, ids, slots, weights, acts, bucket):
    tok_rows, width = acts.shape
    outs = [
        jax.ShapeDtypeStruct((bucket // CAP, CAP, width + PAD), jnp.bfloat16),
        jax.ShapeDtypeStruct((bucket, tok_rows), jnp.bfloat16),
        jax.ShapeDtypeStruct((bucket, 128), jnp.float32),
    ]
    ids, slots, weights, acts = (
        pltpu.with_memory_space_constraint(v, pltpu.HBM) for v in (ids, slots, weights, acts)
    )
    return pl.pallas_call(
        rows_kernel,
        in_specs=[SMEM()] + [pl.BlockSpec(memory_space=pltpu.HBM) for _ in range(4)],
        out_specs=[VMEM() for _ in outs],
        out_shape=outs,
        scratch_shapes=[pltpu.VMEM(v.shape, v.dtype) for v in (ids, slots, weights, acts)]
        + [pltpu.VMEM((bucket, width + PAD), jnp.float32), pltpu.SemaphoreType.DMA((4,))],
        compiler_params=pltpu.CompilerParams(vmem_limit_bytes=16 << 20),
    )(prompt, ids, slots, weights, acts)


def pack_kernel(own, zown, left0, left1, right0, right1, out, total):
    blocks, n, _ = out.shape
    h = left0.shape[0]
    total[...] = own[...].astype(jnp.float32) + zown[...].astype(jnp.float32)
    for i, (left, right) in enumerate(((left0, right0), (left1, right1))):
        side = left[...].astype(jnp.float32) + right[...].astype(jnp.float32)
        total[i * h : (i + 1) * h, :] = total[i * h : (i + 1) * h, :] + side
    skip = blocks - total.shape[0] // n
    for i in range(blocks):
        if i < skip:
            out[i] = jnp.zeros(out.shape[1:], jnp.bfloat16)
        else:
            out[i] = total[(i - skip) * n : (i - skip + 1) * n, :].astype(jnp.bfloat16)


def pack(own, *others):
    rows, width = own.shape
    blocks = lax.axis_size("expert")
    return pl.pallas_call(
        pack_kernel,
        in_specs=[VMEM() for _ in range(6)],
        out_specs=VMEM(),
        out_shape=jax.ShapeDtypeStruct((blocks, CAP, width), jnp.bfloat16),
        scratch_shapes=[pltpu.VMEM((rows, width), jnp.float32)],
        compiler_params=pltpu.CompilerParams(vmem_limit_bytes=16 << 20),
    )(own, *others)


def unpack_kernel(blocks, *refs):
    outs, total = refs[:-1], refs[-1]
    n = blocks.shape[1]
    skip = blocks.shape[0] - total.shape[0] // n
    for i in range(skip, blocks.shape[0]):
        total[(i - skip) * n : (i - skip + 1) * n, :] = blocks[i].astype(jnp.float32)
    h = outs[0].shape[0]
    for i, out in enumerate(outs):
        out[...] = total[i * h : (i + 1) * h, :].astype(jnp.bfloat16)


def unpack(blocks, rows):
    width = blocks.shape[2]
    return pl.pallas_call(
        unpack_kernel,
        in_specs=[VMEM()],
        out_specs=[VMEM(), VMEM()],
        out_shape=[jax.ShapeDtypeStruct((rows // 2, width), jnp.bfloat16) for _ in range(2)],
        scratch_shapes=[pltpu.VMEM((rows, width), jnp.float32)],
        compiler_params=pltpu.CompilerParams(vmem_limit_bytes=16 << 20),
    )(blocks)


def home_kernel(grads, pick, gain, blocks, out, total):
    n = blocks.shape[1]
    factor = gain[:, :1] * grads[lax.axis_index("dp")]
    for i in range(blocks.shape[0]):
        total[i * n : (i + 1) * n, :] = blocks[i].astype(jnp.float32)
    for k in range(0, out.shape[1], CHUNK):
        rows = (total[:, k : k + CHUNK] * factor).astype(jnp.bfloat16)
        grad = lax.dot_general(pick[...], rows, (((0,), (0,)), ((), ())), preferred_element_type=jnp.float32)
        out[:, k : k + CHUNK] = grad.astype(jnp.bfloat16)


def to_tokens(grads, pick, gain, blocks):
    width = blocks.shape[2]
    return pl.pallas_call(
        home_kernel,
        in_specs=[SMEM(), VMEM(), VMEM(), VMEM()],
        out_specs=VMEM(),
        out_shape=jax.ShapeDtypeStruct((pick.shape[1], width), jnp.bfloat16),
        scratch_shapes=[pltpu.VMEM((pick.shape[0], width), jnp.float32)],
        compiler_params=pltpu.CompilerParams(vmem_limit_bytes=16 << 20),
    )(grads, pick, gain, blocks)


def sequence(place, core):
    here = lax.axis_index("dp")
    step, mask = place
    return lax.rem(lax.div(here, 4) + step + 4, 4) * 4 + (lax.rem(here, 4) ^ (mask + core))


def forward_kernel(places, *refs):
    pieces, (w, lever_own, lever_other, before) = refs[:8], refs[8:12]
    flat, own_slope, other_slope, slope16, partial, acc = refs[12:]
    n = pieces[0].shape[0]
    width = w.shape[0]
    half = w.shape[1] // 4
    for i, piece in enumerate(pieces):
        flat[i * n : (i + 1) * n, :] = piece[...]
    for k in range(0, width, CHUNK):
        part = jnp.dot(flat[:, k : k + CHUNK], w[k : k + CHUNK, :], preferred_element_type=jnp.float32)
        acc[...] = part if k == 0 else acc[...] + part
    gain = jnp.sum(flat[:, width:].astype(jnp.float32), axis=1, keepdims=True)
    term = 0.0
    for k, lever_ref, out in ((0, lever_own, own_slope), (1, lever_other, other_slope)):
        lever = lever_ref[...]
        gate = acc[:, 2 * k * half : (2 * k + 1) * half]
        upper = acc[:, (2 * k + 1) * half : (2 * k + 2) * half]
        sig = jax.nn.sigmoid(gate)
        active = gate * sig
        term = term + jnp.sum(active * upper * lever, axis=1, keepdims=True)
        d_gate = lever * upper * sig * (1.0 + gate * (1.0 - sig))
        d_up = lever * active
        out[:, :half] = d_gate
        out[:, half:] = d_up
        slope16[:, 2 * k * half : (2 * k + 1) * half] = d_gate.astype(jnp.bfloat16)
        slope16[:, (2 * k + 1) * half : (2 * k + 2) * half] = d_up.astype(jnp.bfloat16)
    scored = gain * term
    lane = lax.broadcasted_iota(jnp.int32, (1, 128), 1)
    total = before[...]
    for i, place in enumerate(places):
        block = jnp.sum(scored[i * n : (i + 1) * n, :], axis=0, keepdims=True)
        total = total + jnp.where(lane == sequence(place, 0), block, 0.0)
    partial[...] = total


def forward(places, pieces, w, lever_own, lever_other, before):
    n, padded = pieces[0].shape
    rows, half = 8 * n, w.shape[1] // 4
    return pl.pallas_call(
        functools.partial(forward_kernel, places),
        in_specs=[VMEM() for _ in range(12)],
        out_specs=[VMEM() for _ in range(5)],
        out_shape=[
            jax.ShapeDtypeStruct((rows, padded), jnp.bfloat16),
            jax.ShapeDtypeStruct((rows, 2 * half), jnp.float32),
            jax.ShapeDtypeStruct((rows, 2 * half), jnp.float32),
            jax.ShapeDtypeStruct((rows, 4 * half), jnp.bfloat16),
            jax.ShapeDtypeStruct((1, 128), jnp.float32),
        ],
        scratch_shapes=[pltpu.VMEM((rows, 4 * half), jnp.float32)],
        compiler_params=pltpu.CompilerParams(vmem_limit_bytes=32 << 20),
    )(*pieces, w, lever_own, lever_other, before)


def back_kernel(slope, w, *outs):
    for k in range(0, w.shape[0], CHUNK):
        y = lax.dot_general(
            slope[...], w[k : k + CHUNK, :], (((1,), (1,)), ((), ())), preferred_element_type=jnp.float32
        )
        start = 0
        for out in outs:
            out[:, k : k + CHUNK] = y[start : start + out.shape[0], :].astype(jnp.bfloat16)
            start += out.shape[0]


def back(slope, w, sizes):
    return pl.pallas_call(
        back_kernel,
        in_specs=[VMEM(), VMEM()],
        out_specs=[VMEM() for _ in sizes],
        out_shape=[jax.ShapeDtypeStruct((n, w.shape[0]), jnp.bfloat16) for n in sizes],
        compiler_params=pltpu.CompilerParams(vmem_limit_bytes=32 << 20),
    )(slope, w)


def weights_kernel(sources, grads, *refs):
    count = len(sources)
    rows, gains, slopes = refs[:count], refs[count : 2 * count], refs[2 * count : 3 * count]
    gate_out, up_out, scaled = refs[3 * count :]
    half = gate_out.shape[1]

    @pl.when(pl.program_id(0) == 0)
    def _():
        for j, (places, core) in enumerate(sources):
            gain = jnp.sum(gains[j][...].astype(jnp.float32), axis=1, keepdims=True)
            h = gain.shape[0] // len(places)
            factor = jnp.concatenate(
                [gain[i * h : (i + 1) * h, :] * grads[sequence(place, core)] for i, place in enumerate(places)], axis=0
            )
            scaled[j] = (slopes[j][...] * factor).T.astype(jnp.bfloat16)

    total = jnp.zeros((2 * half, gate_out.shape[0]), jnp.float32)
    for j in range(count):
        total = total + jnp.dot(scaled[j], rows[j][...], preferred_element_type=jnp.float32)
    gate_out[...] = total[:half].astype(jnp.bfloat16).T
    up_out[...] = total[half:].astype(jnp.bfloat16).T


def weight_grads(sources, rows, slopes, grads, width, half):
    n = rows[0].shape[0]
    last = width // PAD
    return pl.pallas_call(
        functools.partial(weights_kernel, sources),
        grid=(width // CHUNK,),
        in_specs=[SMEM()]
        + [pl.BlockSpec((n, CHUNK), lambda i: (0, i)) for _ in rows]
        + [pl.BlockSpec((n, PAD), lambda i: (0, last)) for _ in rows]
        + [pl.BlockSpec((n, 2 * half), lambda i: (0, 0)) for _ in slopes],
        out_specs=[pl.BlockSpec((CHUNK, half), lambda i: (i, 0)) for _ in range(2)],
        out_shape=[jax.ShapeDtypeStruct((width, half), jnp.bfloat16) for _ in range(2)],
        scratch_shapes=[pltpu.VMEM((len(rows), 2 * half, n), jnp.bfloat16)],
        compiler_params=pltpu.CompilerParams(vmem_limit_bytes=16 << 20),
    )(grads, *rows, *rows, *slopes)


def shift_x(v, step):
    return lax.ppermute(v, "dp", [(s, ((s // 4 + step) % 4) * 4 + s % 4) for s in range(16)])


def swap(v, axis, mask):
    return lax.ppermute(v, axis, [(s, s ^ mask) for s in range(16)])


def swap_z(v):
    return swap(v, "dp", 2)


def swap_core(v):
    return swap(v, "dp", 1)


def add(*parts):
    total = parts[0].astype(jnp.float32)
    for part in parts[1:]:
        total = total + part.astype(jnp.float32)
    return total.astype(jnp.bfloat16)


def sum_step(v, axis, unit):
    one, two, three = (swap(v, axis, unit * k) for k in (1, 2, 3))
    return (v + one) + (two + three)


def gather_rows(own0, own1):
    left0, right1, zown1 = shift_x(own0, 1), shift_x(own1, -1), swap_z(own1)
    left1, right0, zown0 = shift_x(own1, 1), shift_x(own0, -1), swap_z(own0)
    far0, far1 = shift_x(left0, 1), shift_x(right1, -1)
    zleft0, zright1 = swap_z(left0), swap_z(right1)
    zleft1, zright0 = shift_x(zown1, 1), shift_x(zown0, -1)
    zfar0, zfar1 = shift_x(zleft0, 1), shift_x(zright1, -1)
    first = [own0, own1, left0, left1, right0, right1, zown0, zown1]
    second = [far0, zleft1, far1, zright0, zleft0, zright1, zfar0, zfar1]
    return first, second


def reduce_rows(make_first, second, later):
    plus, minus, across, zfar0, zfar1 = second
    h = zfar0.shape[0]
    zfar0, zfar1, later = lax.optimization_barrier((zfar0, zfar1, later))
    got0 = shift_x(zfar0, -1)
    got1 = shift_x(zfar1, 1)
    got_plus = shift_x(plus, -1)
    got_minus = shift_x(minus, 1)
    later = sum_step(later, "dp", 1)
    got0, got1, later = lax.optimization_barrier((got0, got1, later))
    later = sum_step(later, "expert", 4)
    across = add(across, jnp.concatenate([got0, got1], axis=0))
    across, later = lax.optimization_barrier((across, later))
    got_across = swap_z(across)
    own, left0, left1, right0, right1, zown = make_first(across)
    got_left1, got_right0 = shift_x(left1, -1), shift_x(right0, 1)
    own, later = lax.optimization_barrier((own, later))
    later = sum_step(later, "expert", 1)
    got_plus, got_minus = lax.optimization_barrier((got_plus, got_minus))
    got_across, got_left1, got_right0 = lax.optimization_barrier((got_across, got_left1, got_right0))
    zown = jnp.concatenate([add(zown[:h], got_minus[h:]), add(zown[h:], got_plus[h:])], axis=0)
    got_zown = swap_z(zown)
    left0 = add(left0, got_plus[:h], got_across[:h])
    right1 = add(right1, got_minus[:h], got_across[h:])
    left0, right1 = lax.optimization_barrier((left0, right1))
    sums = (got_zown, shift_x(left0, -1), got_left1, got_right0, shift_x(right1, 1))
    *sums, later = lax.optimization_barrier((*sums, later))
    return pack(own, *sums), later


FIRST = ((0, 0), (0, 0), (-1, 0), (-1, 0), (1, 0), (1, 0), (0, 2), (0, 2))
SECOND = ((2, 0), (-1, 2), (2, 0), (1, 2), (-1, 2), (1, 2), (2, 2), (2, 2))


def per_device(
    tokens,
    expert_ids,
    slots,
    route_weights,
    w_gate,
    w_up,
    w_down,
    readout,
    ref_scores,
    partner,
    prompt_len,
):
    n_exp = lax.axis_size("expert")
    row_index = lax.axis_index("dp")
    acts = tokens[0]
    tok_rows, width = acts.shape
    outgoing, token_pick, slot_gain = make_rows(
        prompt_len, expert_ids[0].T, slots[0].T, route_weights[0].T, acts, n_exp * CAP
    )

    def to_experts(v):
        return lax.all_to_all(v, "expert", split_axis=0, concat_axis=0, tiled=True)

    half = w_gate.shape[2]
    gate_other, up_other = swap_core(w_gate[0]), swap_core(w_up[0])
    lever_own = jnp.dot(w_down[0], readout, preferred_element_type=jnp.float32)
    lever_own = lever_own.reshape(1, half)
    lever_other = swap_core(lever_own)
    w_all = jnp.concatenate([w_gate[0], w_up[0], gate_other, up_other], axis=1)
    blocks, w_all, lever_own, lever_other = lax.optimization_barrier(
        (to_experts(outgoing), w_all, lever_own, lever_other)
    )
    mine = unpack(blocks, (n_exp - PROMPT_MIN // tok_rows) * CAP)

    pieces = gather_rows(*mine)
    unit = 2 * mine[0].shape[0]
    partial = jnp.zeros((1, 128), jnp.float32)
    slopes16, sources, rows, slopes = [], [], [], []
    for some, places in zip(pieces, (FIRST, SECOND)):
        flat, own_slope, other_slope, slope16, partial = forward(places, some, w_all, lever_own, lever_other, partial)
        slopes16.append(slope16)
        sources += [(places, 0), (places, 1)]
        rows += [flat, swap_core(flat)]
        slopes += [own_slope, swap_core(other_slope)]

    def make_first(after):
        slope, _ = lax.optimization_barrier((slopes16[0], after))
        return back(slope, w_all, [unit] + [unit // 2] * 4 + [unit])

    packed, partial = reduce_rows(make_first, back(slopes16[1], w_all, [unit] * 3 + [unit // 2] * 2), partial)
    packed, later = lax.optimization_barrier((packed, partial))
    scores = sum_step(later, "dp", 4)[0, : partner.shape[0]]
    losses, grads = preference(scores, ref_scores, partner)
    gate_grads, up_grads = weight_grads(sources, rows, slopes, grads, width, half)
    home, gate_grads, up_grads = lax.optimization_barrier((to_experts(packed), gate_grads, up_grads))
    token_grads = to_tokens(grads, token_pick, slot_gain, home)
    return (token_grads[None], gate_grads[None], up_grads[None], losses)


def solution(mesh):
    placed = (
        P("dp", "expert", None),
        P("dp", "expert", None),
        P("dp", "expert", None),
        P("dp", "expert", None),
        P("expert", None, "dp"),
        P("expert", None, "dp"),
        P("expert", "dp", None),
        P(),
        P(),
        P(),
        P(),
    )
    return jax.shard_map(
        per_device,
        mesh=mesh,
        in_specs=placed,
        out_specs=(P("dp", "expert", None), P("expert", None, "dp"), P("expert", None, "dp"), P()),
        check_vma=False,
    )
```
